32 devices in a mesh: seq: 8 (over y, x, core), shard: 4 (over z).
Axes of the slice: x: 2, y: 2, z: 4, core: 2. Of those that a mesh axis runs over, the one named last changes fastest.
Arguments:
- residual_in: bfloat16 [8192, 640], P(('seq', 'shard')), may hold values from -6 to 6
- cotangent: float32 [8192, 640], P(('seq', 'shard')), may hold values from -6 to 6
- qkv_weight: bfloat16 [1536, 640], P(('seq', 'shard')), may hold values from -0.25 to 0.25
- out_weight: bfloat16 [1024, 640], P(('seq', 'shard')), may hold values from -0.1875 to 0.1875
- mlp_weight: bfloat16 [2048, 1920], P(('seq', 'shard')), may hold values from -0.25 to 0.25
- norm_gains: bfloat16 [3072], P(('seq', 'shard')), may hold values from -0.5 to 0.5
- seq_offsets: int32 [8192], P(('seq', 'shard')), may hold values from 0 to 1023, as said below
- positions: int32 [8192], P(('seq', 'shard')), may hold values from 0 to 2046, as said below
Outputs:
- block_out: bfloat16 [8192, 640], P(('seq', 'shard'))
- grad_input: float32 [8192, 640], P(('seq', 'shard'))
- grad_qkv: float32 [1536, 640], P(('seq', 'shard'))
- grad_out: float32 [1024, 640], P(('seq', 'shard'))
- grad_mlp: float32 [2048, 1920], P(('seq', 'shard'))
- grad_gains: float32 [3072], P(('seq', 'shard'))
The draws below stay inside these ranges and needn't reach their ends.
Inputs may be any that keep to these rules, and one draw needn't show every extreme that they name: Sequences are runs of consecutive tokens, 256 to 1024 long (the last may be cut shorter); the first is 1024 long; seq_offsets counts up from 0 along each sequence. Within a sequence, positions rise by 1 or 2 from token to token; the first sequence starts at 0 and rises by 2 throughout; a sequence of n tokens starts at most at 2 * (1024 - n).
All inputs are finite; a program needn't handle non-finite values.
Results may differ from the reference program's by a relative error of at most 0.017.
Values may be sent and summed in bfloat16 or wider, within the bound.
No kernel may reach another device: no remote copies, remote signals or barrier semaphores. Data moves between devices by JAX's collectives and lax.ppermute only.
A program may use at most 128 MiB of HBM per device.

```python
import math
import jax
import jax.numpy as jnp
from jax import lax

D = 640
HEADS = 4
HEAD_DIM = 256
FF = 2048
WINDOW = 512
SEQ_LEN = 1024
TOK_DEV = 256
TOKENS = 8192


def sequence_layout(key):
    length_count = TOKENS // (SEQ_LEN // 4) + 2
    lengths = jax.random.randint(jax.random.fold_in(key, 11), (length_count,), SEQ_LEN // 4, SEQ_LEN + 1)
    lengths = lengths.at[0].set(SEQ_LEN)
    starts = jnp.cumsum(lengths) - lengths
    marks = jnp.zeros((TOKENS,), jnp.int32).at[starts].set(1, mode='drop')
    index_all = jnp.arange(TOKENS, dtype=jnp.int32)
    first_token = lax.cummax(jnp.where(marks == 1, index_all, 0), axis=0)
    offsets = index_all - first_token
    segment_id = jnp.cumsum(marks) - 1
    base_limit = 2 * (SEQ_LEN - lengths) + 1
    bases = jax.random.randint(jax.random.fold_in(key, 12), (length_count,), 0, base_limit)
    bases = bases.at[0].set(0)
    increments = jax.random.randint(jax.random.fold_in(key, 13), (TOKENS,), 1, 3)
    increments = jnp.where(index_all < SEQ_LEN, 2, increments)
    climbing = jnp.cumsum(increments)
    position_ids = bases[segment_id] + climbing - climbing[first_token]
    return (offsets.astype(jnp.int32), position_ids.astype(jnp.int32))


def draw_seq_offsets(key, part):
    return sequence_layout(key)[0]


def draw_positions(key, part):
    return sequence_layout(key)[1]


def block_scale(key, extent, cuts, low, top_value):
    factor_of = 1.0
    for axis_at, blocks in cuts:
        heights = jax.random.uniform(jax.random.fold_in(jax.random.fold_in(key, 6), axis_at), (blocks,), jnp.float32, low / len(cuts), top_value / len(cuts))
        factor_of = factor_of * jnp.repeat(jnp.exp(heights), extent[axis_at] // blocks).reshape((-1,) + (1,) * (len(extent) - 1 - axis_at))
    return factor_of


def normal_values(rng, dims, width, reach, split=(), kind=jnp.bfloat16):
    loudness = block_scale(rng, dims, split, -0.22, 0.18) if split else 1.0
    drawn = jax.random.normal(rng, dims, jnp.float32) * width * loudness
    return jnp.minimum(jnp.maximum(drawn, -reach), reach).astype(kind)


def setup_inputs(seed: int = 0) -> dict:
    key_list = jax.random.split(jax.random.key(seed), 9)
    residual_in = normal_values(key_list[0], (TOKENS, D), 1.0, 6.0, ((0, 32),))
    cotangent = normal_values(key_list[1], (TOKENS, D), 1.0, 6.0, ((0, 32),), jnp.float32)
    qkv_weight = normal_values(key_list[2], ((HEADS + 2) * HEAD_DIM, D), D ** -0.5, 0.25, ((0, 32),))
    out_weight = normal_values(key_list[3], (HEADS * HEAD_DIM, D), (HEADS * HEAD_DIM) ** -0.5, 0.1875, ((0, 32),))
    mlp_weight = normal_values(key_list[4], (FF, 3 * D), D ** -0.5, 0.25, ((0, 32),))
    norm_gains = jnp.clip(jax.random.uniform(key_list[5], (4 * D + 2 * HEAD_DIM,), jnp.float32, -0.5, 0.5) * block_scale(key_list[5], (4 * D + 2 * HEAD_DIM,), ((0, 32),), -0.4, 0.0), -0.5, 0.5).astype(jnp.bfloat16)
    seq_offsets = draw_seq_offsets(jax.random.fold_in(key_list[8], 71), 0)
    positions = draw_positions(jax.random.fold_in(key_list[8], 71), 0)
    return dict(residual_in=residual_in, cotangent=cotangent, qkv_weight=qkv_weight, out_weight=out_weight, mlp_weight=mlp_weight, norm_gains=norm_gains, seq_offsets=seq_offsets, positions=positions)


EPSILON = 1e-06
ROPE_BASE = 10000.0
GELU_SCALE = 0.7978845608028654
GELU_CUBIC = 0.044715

def norm_rows(values, gain_vec):
    inv_rms = lax.rsqrt(lax.optimization_barrier(jnp.mean(values * values, axis=-1, keepdims=True)) + EPSILON)
    return (values * inv_rms * (1.0 + gain_vec), inv_rms)

def norm_back(values, inv_rms, gain_vec, upstream):
    weighted = upstream * (1.0 + gain_vec)
    inner = lax.optimization_barrier(jnp.mean(weighted * values, axis=-1, keepdims=True))
    return (inv_rms * weighted - values * (inv_rms * inv_rms * inv_rms) * inner, upstream * values * inv_rms)

def gelu_value(values):
    return 0.5 * values * (1.0 + jnp.tanh(GELU_SCALE * (values + GELU_CUBIC * values * values * values)))

def gelu_slope(values):
    tangent = jnp.tanh(GELU_SCALE * (values + GELU_CUBIC * values * values * values))
    return 0.5 * (1.0 + tangent) + 0.5 * values * (1.0 - tangent * tangent) * GELU_SCALE * (1.0 + 3.0 * GELU_CUBIC * values * values)

def rope_tables(position_ids, head_dim):
    half_dim = head_dim // 2
    exponent = jnp.arange(half_dim, dtype=jnp.float32) * (-2.0 / head_dim)
    frequency = jnp.power(jnp.float32(ROPE_BASE), exponent)
    angle = position_ids.astype(jnp.float32)[:, None] * frequency[None, :]
    return (jnp.cos(angle), jnp.sin(angle))

def rotate(values, cosine, sine_table):
    half_dim = values.shape[-1] // 2
    first_half = values[..., :half_dim]
    second_half = values[..., half_dim:]
    cos_wide = cosine[:, None, :]
    sine_wide = sine_table[:, None, :]
    return jnp.concatenate([first_half * cos_wide - second_half * sine_wide, second_half * cos_wide + first_half * sine_wide], axis=-1)

def unrotate(upstream, cosine, sine_table):
    half_dim = upstream.shape[-1] // 2
    first_half = upstream[..., :half_dim]
    second_half = upstream[..., half_dim:]
    cos_wide = cosine[:, None, :]
    sine_wide = sine_table[:, None, :]
    return jnp.concatenate([first_half * cos_wide + second_half * sine_wide, second_half * cos_wide - first_half * sine_wide], axis=-1)

def window_mask(offset_blk, query_count, window):
    row_index = jnp.arange(query_count, dtype=jnp.int32)[:, None]
    col_index = jnp.arange(window + query_count, dtype=jnp.int32)[None, :]
    distance = row_index + window - col_index
    return (distance >= 0) & (distance < window) & (distance <= offset_blk[:, None])

def attend(query_blk, key_value, offset_blk, head_dim):
    query_count = query_blk.shape[0]
    head_count = query_blk.shape[1] // head_dim
    key_rows = key_value[:, :head_dim]
    value_rows = key_value[:, head_dim:]
    flat_query = query_blk.reshape(query_count * head_count, head_dim)
    scores = jnp.dot(flat_query, key_rows.T, preferred_element_type=jnp.float32).reshape(query_count, head_count, -1) * head_dim ** (-0.5)
    visible = window_mask(offset_blk, query_count, key_value.shape[0] - query_count)[:, None, :]
    log_total = jnp.log(lax.optimization_barrier(jnp.sum(jnp.where(visible, jnp.exp(scores), 0.0), axis=-1)))
    attn_probs = jnp.where(visible, jnp.exp(scores - log_total[:, :, None]), 0.0).astype(jnp.bfloat16)
    attended = jnp.dot(attn_probs.reshape(query_count * head_count, -1), value_rows, preferred_element_type=jnp.float32)
    return (attended.reshape(query_count, head_count * head_dim).astype(jnp.bfloat16), log_total)

def attend_back(query_blk, key_value, offset_blk, log_total, upstream_blk, head_dim):
    query_count = query_blk.shape[0]
    head_count = query_blk.shape[1] // head_dim
    key_rows = key_value[:, :head_dim]
    value_rows = key_value[:, head_dim:]
    flat_query = query_blk.reshape(query_count * head_count, head_dim)
    flat_upstream = upstream_blk.reshape(query_count * head_count, head_dim)
    scale_value = head_dim ** (-0.5)
    scores = jnp.dot(flat_query, key_rows.T, preferred_element_type=jnp.float32).reshape(query_count, head_count, -1) * scale_value
    visible = window_mask(offset_blk, query_count, key_value.shape[0] - query_count)[:, None, :]
    attn_probs = jnp.where(visible, jnp.exp(scores - log_total[:, :, None]), 0.0)
    probs_low = attn_probs.astype(jnp.bfloat16).reshape(query_count * head_count, -1)
    grad_probs = jnp.dot(flat_upstream, value_rows.T, preferred_element_type=jnp.float32).reshape(query_count, head_count, -1)
    delta_sum = lax.optimization_barrier(jnp.sum(attn_probs * grad_probs, axis=-1, keepdims=True))
    grad_scores = (attn_probs * (grad_probs - delta_sum) * scale_value).astype(jnp.bfloat16)
    flat_scores = grad_scores.reshape(query_count * head_count, -1)
    grad_query = jnp.dot(flat_scores, key_rows, preferred_element_type=jnp.float32).reshape(query_count, head_count * head_dim)
    grad_keys = jnp.dot(flat_scores.T, flat_query, preferred_element_type=jnp.float32)
    grad_values = jnp.dot(probs_low.T, flat_upstream, preferred_element_type=jnp.float32)
    return (grad_query, jnp.concatenate([grad_keys, grad_values], axis=1))

def reference(residual_in, cotangent, qkv_weight, out_weight, mlp_weight, norm_gains, seq_offsets, positions):
    head_dim = HEAD_DIM
    query_width = HEADS * head_dim
    gain_vals = norm_gains.astype(jnp.float32)
    gain_in = gain_vals[0:D]
    gain_post = gain_vals[D:2 * D]
    gain_pre = gain_vals[2 * D:3 * D]
    gain_ff = gain_vals[3 * D:4 * D]
    gain_query = gain_vals[4 * D:4 * D + head_dim]
    gain_key = gain_vals[4 * D + head_dim:]
    row_block = math.gcd(TOKENS, 4096)
    row_blocks = TOKENS // row_block
    query_block = min(TOK_DEV, 256)
    query_blocks = TOKENS // query_block
    gate_w = mlp_weight[:, :D]
    up_w = mlp_weight[:, D:2 * D]
    down_w = mlp_weight[:, 2 * D:]

    def split_qkv(normed_in, pos_blk):
        projected_qkv = jnp.dot(normed_in, qkv_weight.T, preferred_element_type=jnp.float32)
        query_raw = projected_qkv[:, :query_width].reshape(-1, HEADS, head_dim)
        key_raw = projected_qkv[:, query_width:query_width + head_dim]
        value_raw = projected_qkv[:, query_width + head_dim:]
        cosine, sine_table = rope_tables(pos_blk, head_dim)
        return (query_raw, key_raw, value_raw, cosine, sine_table)

    def section_front(inputs):
        x_blk, pos_blk = inputs
        normed_in, _ = norm_rows(x_blk.astype(jnp.float32), gain_in)
        normed_in = normed_in.astype(jnp.bfloat16)
        query_raw, key_raw, value_raw, cosine, sine_table = split_qkv(normed_in, pos_blk)
        query_norm, _ = norm_rows(query_raw, gain_query)
        key_norm, _ = norm_rows(key_raw, gain_key)
        queries = rotate(query_norm, cosine, sine_table).reshape(row_block, query_width).astype(jnp.bfloat16)
        key_rot = rotate(key_norm[:, None, :], cosine, sine_table)[:, 0, :]
        key_value = jnp.concatenate([key_rot, value_raw], axis=1).astype(jnp.bfloat16)
        return (normed_in, queries, key_value)
    normed_all, queries_all, kv_all = lax.map(section_front, (residual_in.reshape(row_blocks, row_block, D), positions.reshape(row_blocks, row_block)))
    normed_all = normed_all.reshape(TOKENS, D)
    queries_all = queries_all.reshape(TOKENS, query_width)
    kv_all = kv_all.reshape(TOKENS, 2 * head_dim)
    kv_padded = jnp.concatenate([jnp.zeros((WINDOW, 2 * head_dim), jnp.bfloat16), kv_all], axis=0)

    def attend_block(block_index):
        row_start = block_index * query_block
        query_blk = lax.dynamic_slice_in_dim(queries_all, row_start, query_block, 0)
        kv_blk = lax.dynamic_slice_in_dim(kv_padded, row_start, WINDOW + query_block, 0)
        offset_blk = lax.dynamic_slice_in_dim(seq_offsets, row_start, query_block, 0)
        return attend(query_blk, kv_blk, offset_blk, head_dim)
    attended_all, totals_all = lax.map(attend_block, jnp.arange(query_blocks, dtype=jnp.int32))
    attended_all = attended_all.reshape(TOKENS, query_width)
    totals_all = totals_all.reshape(TOKENS, HEADS)

    def section_middle(running, inputs):
        acc_out, acc_mlp, acc_post, acc_pre, acc_ff = running
        x_blk, attended_blk, upstream = inputs
        projected = jnp.dot(attended_blk, out_weight, preferred_element_type=jnp.float32)
        branch, rms_post = norm_rows(projected, gain_post)
        midstream = x_blk.astype(jnp.float32) + branch
        normed_mid, rms_mid = norm_rows(midstream, gain_pre)
        normed_mid = normed_mid.astype(jnp.bfloat16)
        gate_out = jnp.dot(normed_mid, gate_w.T, preferred_element_type=jnp.float32)
        up_out = jnp.dot(normed_mid, up_w.T, preferred_element_type=jnp.float32)
        activated = gelu_value(gate_out)
        hidden = (activated * up_out).astype(jnp.bfloat16)
        mlp_out = jnp.dot(hidden, down_w, preferred_element_type=jnp.float32)
        ff_branch, rms_ff = norm_rows(mlp_out, gain_ff)
        block_out = (midstream + ff_branch).astype(jnp.bfloat16)
        grad_mlp_out, term_ff = norm_back(mlp_out, rms_ff, gain_ff, upstream)
        grad_mlp_b = grad_mlp_out.astype(jnp.bfloat16)
        grad_hidden = jnp.dot(grad_mlp_b, down_w.T, preferred_element_type=jnp.float32)
        grad_gate = (grad_hidden * up_out * gelu_slope(gate_out)).astype(jnp.bfloat16)
        grad_up = (grad_hidden * activated).astype(jnp.bfloat16)
        grad_mid = jnp.dot(grad_gate, gate_w, preferred_element_type=jnp.float32) + jnp.dot(grad_up, up_w, preferred_element_type=jnp.float32)
        grad_mid_in, term_pre = norm_back(midstream, rms_mid, gain_pre, grad_mid)
        grad_midstream = upstream + grad_mid_in
        grad_proj, term_post = norm_back(projected, rms_post, gain_post, grad_midstream)
        grad_proj_b = grad_proj.astype(jnp.bfloat16)
        grad_attended = jnp.dot(grad_proj_b, out_weight.T, preferred_element_type=jnp.float32).astype(jnp.bfloat16)
        acc_out = acc_out + jnp.dot(attended_blk.T, grad_proj_b, preferred_element_type=jnp.float32)
        mlp_term = jnp.concatenate([jnp.dot(grad_gate.T, normed_mid, preferred_element_type=jnp.float32), jnp.dot(grad_up.T, normed_mid, preferred_element_type=jnp.float32), jnp.dot(hidden.T, grad_mlp_b, preferred_element_type=jnp.float32)], axis=1)
        acc_mlp = acc_mlp + mlp_term
        acc_post = acc_post + lax.optimization_barrier(jnp.sum(term_post, axis=0))
        acc_pre = acc_pre + lax.optimization_barrier(jnp.sum(term_pre, axis=0))
        acc_ff = acc_ff + lax.optimization_barrier(jnp.sum(term_ff, axis=0))
        return ((acc_out, acc_mlp, acc_post, acc_pre, acc_ff), (block_out, grad_midstream, grad_attended))
    middle_init = (jnp.zeros((query_width, D), jnp.float32), jnp.zeros((FF, 3 * D), jnp.float32), jnp.zeros((D,), jnp.float32), jnp.zeros((D,), jnp.float32), jnp.zeros((D,), jnp.float32))
    middle_acc, middle_out = lax.scan(section_middle, middle_init, (residual_in.reshape(row_blocks, row_block, D), attended_all.reshape(row_blocks, row_block, query_width), cotangent.reshape(row_blocks, row_block, D)))
    grad_out, grad_mlp, sum_post, sum_pre, sum_ff = middle_acc
    block_out = middle_out[0].reshape(TOKENS, D)
    grad_mid_all = middle_out[1]
    grad_att_all = middle_out[2].reshape(TOKENS, query_width)

    def attend_back_block(running, block_index):
        row_start = block_index * query_block
        query_blk = lax.dynamic_slice_in_dim(queries_all, row_start, query_block, 0)
        kv_blk = lax.dynamic_slice_in_dim(kv_padded, row_start, WINDOW + query_block, 0)
        offset_blk = lax.dynamic_slice_in_dim(seq_offsets, row_start, query_block, 0)
        total_blk = lax.dynamic_slice_in_dim(totals_all, row_start, query_block, 0)
        upstream_blk = lax.dynamic_slice_in_dim(grad_att_all, row_start, query_block, 0)
        grad_query, grad_kv = attend_back(query_blk, kv_blk, offset_blk, total_blk, upstream_blk, head_dim)
        current = lax.dynamic_slice_in_dim(running, row_start, WINDOW + query_block, 0) + grad_kv
        running = lax.dynamic_update_slice_in_dim(running, current, row_start, 0)
        return (running, grad_query)
    grad_kv_padded, grad_query_all = lax.scan(attend_back_block, jnp.zeros((WINDOW + TOKENS, 2 * head_dim), jnp.float32), jnp.arange(query_blocks, dtype=jnp.int32))
    grad_kv_all = grad_kv_padded[WINDOW:]
    grad_query_all = grad_query_all.reshape(TOKENS, query_width)

    def section_back(running, inputs):
        acc_qkv, acc_in, acc_query, acc_key = running
        x_blk, normed_in, pos_blk, grad_query, grad_kv, grad_midstream = inputs
        query_raw, key_raw, value_raw, cosine, sine_table = split_qkv(normed_in, pos_blk)
        _, rms_query = norm_rows(query_raw, gain_query)
        _, rms_key = norm_rows(key_raw, gain_key)
        grad_qnorm = unrotate(grad_query.reshape(row_block, HEADS, head_dim), cosine, sine_table)
        grad_qraw, term_query = norm_back(query_raw, rms_query, gain_query, grad_qnorm)
        grad_knorm = unrotate(grad_kv[:, None, :head_dim], cosine, sine_table)[:, 0, :]
        grad_kraw, term_key = norm_back(key_raw, rms_key, gain_key, grad_knorm)
        grad_qkv_b = jnp.concatenate([grad_qraw.reshape(row_block, query_width), grad_kraw, grad_kv[:, head_dim:]], axis=1).astype(jnp.bfloat16)
        grad_normed = jnp.dot(grad_qkv_b, qkv_weight, preferred_element_type=jnp.float32)
        input_f32 = x_blk.astype(jnp.float32)
        _, rms_in = norm_rows(input_f32, gain_in)
        grad_in_norm, term_in = norm_back(input_f32, rms_in, gain_in, grad_normed)
        grad_input = grad_midstream + grad_in_norm
        acc_qkv = acc_qkv + jnp.dot(grad_qkv_b.T, normed_in, preferred_element_type=jnp.float32)
        acc_in = acc_in + lax.optimization_barrier(jnp.sum(term_in, axis=0))
        acc_query = acc_query + lax.optimization_barrier(jnp.sum(term_query, axis=(0, 1)))
        acc_key = acc_key + lax.optimization_barrier(jnp.sum(term_key, axis=0))
        return ((acc_qkv, acc_in, acc_query, acc_key), grad_input)
    back_init = (jnp.zeros(((HEADS + 2) * head_dim, D), jnp.float32), jnp.zeros((D,), jnp.float32), jnp.zeros((head_dim,), jnp.float32), jnp.zeros((head_dim,), jnp.float32))
    back_acc, grad_input = lax.scan(section_back, back_init, (residual_in.reshape(row_blocks, row_block, D), normed_all.reshape(row_blocks, row_block, D), positions.reshape(row_blocks, row_block), grad_query_all.reshape(row_blocks, row_block, query_width), grad_kv_all.reshape(row_blocks, row_block, 2 * head_dim), grad_mid_all))
    grad_qkv, sum_in, sum_query, sum_key = back_acc
    grad_gains = jnp.concatenate([sum_in, sum_post, sum_pre, sum_ff, sum_query, sum_key])
    return (block_out, grad_input.reshape(TOKENS, D), grad_qkv, grad_out, grad_mlp, grad_gains)
```

```python
import math
import jax
import jax.numpy as jnp
from jax import lax
from jax.sharding import Mesh, PartitionSpec as P

AXES = ("y", "x", "c", "z")


def split_mesh(mesh):
    slow, fast = mesh.devices.shape
    cores = 2 if slow % 2 == 0 else 1
    chips = slow // cores
    across = max(d for d in range(1, math.isqrt(chips) + 1) if chips % d == 0)
    return Mesh(mesh.devices.reshape(chips // across, across, cores, fast), AXES)


def pass_on(block, axis, step):
    count = lax.axis_size(axis)
    return lax.ppermute(block, axis, [(i, (i + step) % count) for i in range(count)])


def spread(block, axis):
    count = lax.axis_size(axis)
    return jnp.stack([block] + [pass_on(block, axis, d) for d in range(1, count)])


def fold(parts, axis, dtype):
    count = lax.axis_size(axis)
    total = parts[0].astype(jnp.float32)
    for d in range(1, count):
        total = total + pass_on(parts[d], axis, -d).astype(jnp.float32)
    return total.astype(dtype)

HEADS = 4
HEAD_DIM = 256
WINDOW = 512


EPSILON = 1e-06
ROPE_BASE = 10000.0
GELU_SCALE = 0.7978845608028654
GELU_CUBIC = 0.044715


def norm_rows(values, gain_vec):
    inv_rms = lax.rsqrt(jnp.mean(values * values, axis=-1, keepdims=True) + EPSILON)
    return (values * inv_rms * (1.0 + gain_vec), inv_rms)


def norm_back(values, inv_rms, gain_vec, upstream):
    weighted = upstream * (1.0 + gain_vec)
    inner = jnp.mean(weighted * values, axis=-1, keepdims=True)
    return (
        inv_rms * weighted - values * (inv_rms * inv_rms * inv_rms) * inner,
        upstream * values * inv_rms,
    )


def gelu_value(values):
    return (
        0.5
        * values
        * (1.0 + jnp.tanh(GELU_SCALE * (values + GELU_CUBIC * values * values * values)))
    )


def gelu_slope(values):
    tangent = jnp.tanh(GELU_SCALE * (values + GELU_CUBIC * values * values * values))
    return 0.5 * (1.0 + tangent) + 0.5 * values * (1.0 - tangent * tangent) * GELU_SCALE * (
        1.0 + 3.0 * GELU_CUBIC * values * values
    )


def rope_tables(position_ids, head_dim):
    half_dim = head_dim // 2
    exponent = jnp.arange(half_dim, dtype=jnp.float32) * (-2.0 / head_dim)
    frequency = jnp.power(jnp.float32(ROPE_BASE), exponent)
    angle = position_ids.astype(jnp.float32)[:, None] * frequency[None, :]
    return (jnp.cos(angle), jnp.sin(angle))


def rotate(values, cosine, sine_table):
    half_dim = values.shape[-1] // 2
    first_half = values[..., :half_dim]
    second_half = values[..., half_dim:]
    cos_wide = cosine[:, None, :]
    sine_wide = sine_table[:, None, :]
    return jnp.concatenate(
        [
            first_half * cos_wide - second_half * sine_wide,
            second_half * cos_wide + first_half * sine_wide,
        ],
        axis=-1,
    )


def unrotate(upstream, cosine, sine_table):
    half_dim = upstream.shape[-1] // 2
    first_half = upstream[..., :half_dim]
    second_half = upstream[..., half_dim:]
    cos_wide = cosine[:, None, :]
    sine_wide = sine_table[:, None, :]
    return jnp.concatenate(
        [
            first_half * cos_wide + second_half * sine_wide,
            second_half * cos_wide - first_half * sine_wide,
        ],
        axis=-1,
    )


def window_mask(offset_blk, query_count, window):
    row_index = jnp.arange(query_count, dtype=jnp.int32)[:, None]
    col_index = jnp.arange(window + query_count, dtype=jnp.int32)[None, :]
    distance = row_index + window - col_index
    return (distance >= 0) & (distance < window) & (distance <= offset_blk[:, None])


def attend(query_blk, key_value, offset_blk, head_dim):
    query_count = query_blk.shape[0]
    head_count = query_blk.shape[1] // head_dim
    key_rows = key_value[:, :head_dim]
    value_rows = key_value[:, head_dim:]
    flat_query = query_blk.reshape(query_count * head_count, head_dim)
    scores = jnp.dot(flat_query, key_rows.T, preferred_element_type=jnp.float32).reshape(
        query_count, head_count, -1
    ) * head_dim ** (-0.5)
    visible = window_mask(offset_blk, query_count, key_value.shape[0] - query_count)[:, None, :]
    log_total = jnp.log(jnp.sum(jnp.where(visible, jnp.exp(scores), 0.0), axis=-1))
    attn_probs = jnp.where(visible, jnp.exp(scores - log_total[:, :, None]), 0.0).astype(
        jnp.bfloat16
    )
    attended = jnp.dot(
        attn_probs.reshape(query_count * head_count, -1),
        value_rows,
        preferred_element_type=jnp.float32,
    )
    return (attended.reshape(query_count, head_count * head_dim).astype(jnp.bfloat16), log_total)


def attend_back(query_blk, key_value, offset_blk, log_total, upstream_blk, head_dim):
    query_count = query_blk.shape[0]
    head_count = query_blk.shape[1] // head_dim
    key_rows = key_value[:, :head_dim]
    value_rows = key_value[:, head_dim:]
    flat_query = query_blk.reshape(query_count * head_count, head_dim)
    flat_upstream = upstream_blk.reshape(query_count * head_count, head_dim)
    scale_value = head_dim ** (-0.5)
    scores = (
        jnp.dot(flat_query, key_rows.T, preferred_element_type=jnp.float32).reshape(
            query_count, head_count, -1
        )
        * scale_value
    )
    visible = window_mask(offset_blk, query_count, key_value.shape[0] - query_count)[:, None, :]
    attn_probs = jnp.where(visible, jnp.exp(scores - log_total[:, :, None]), 0.0)
    probs_low = attn_probs.astype(jnp.bfloat16).reshape(query_count * head_count, -1)
    grad_probs = jnp.dot(flat_upstream, value_rows.T, preferred_element_type=jnp.float32).reshape(
        query_count, head_count, -1
    )
    delta_sum = jnp.sum(attn_probs * grad_probs, axis=-1, keepdims=True)
    grad_scores = (attn_probs * (grad_probs - delta_sum) * scale_value).astype(jnp.bfloat16)
    flat_scores = grad_scores.reshape(query_count * head_count, -1)
    grad_query = jnp.dot(flat_scores, key_rows, preferred_element_type=jnp.float32).reshape(
        query_count, head_count * head_dim
    )
    grad_keys = jnp.dot(flat_scores.T, flat_query, preferred_element_type=jnp.float32)
    grad_values = jnp.dot(probs_low.T, flat_upstream, preferred_element_type=jnp.float32)
    return (grad_query, jnp.concatenate([grad_keys, grad_values], axis=1))


def shifted(block, axis, distance):
    count = math.prod(lax.axis_size(name) for name in axis)
    devices = range(count)
    route = [(i - distance, i) for i in devices if i - distance in devices]
    return lax.ppermute(block, axis, route)


def order_of(axes_sizes, to_abs):
    index = jnp.zeros((), jnp.int32)
    for name, count in axes_sizes:
        place = lax.rem(lax.axis_index(name) - jnp.arange(count, dtype=jnp.int32) + count, count)
        index = index[..., None] * count + place
    return index.reshape(-1)


def gather_late(shard_a, shard_b):
    rows_a = shard_a.shape[0]
    sizes = {name: lax.axis_size(name) for name in AXES}
    far_a = spread(shard_a, "z")
    half = sizes["z"] // 2
    low, high = far_a[:half], far_a[half:]
    mid_b = spread(spread(shard_b, "x"), "y")
    low = spread(low, "x")
    high = spread(high, "y")
    low = spread(low, "y")
    high = spread(high, "x").swapaxes(0, 1)
    full_b = spread(mid_b, "z")
    full_b = jnp.moveaxis(full_b, 0, 2)
    full_a = jnp.concatenate([low, high], axis=2)
    full_a = spread(full_a, "c")
    full_b = spread(full_b, "c")
    return full_a, full_b


def scatter_a(grads):
    half = lax.axis_size("z") // 2
    own = fold(grads, "c", jnp.bfloat16)
    low, high = own[:, :, :half], own[:, :, half:]
    low = fold(jnp.moveaxis(low, 1, 0), "x", jnp.bfloat16)
    high = fold(high, "y", jnp.bfloat16)
    low = fold(low, "y", jnp.bfloat16)
    high = fold(high, "x", jnp.bfloat16)
    return fold(jnp.concatenate([low, high], axis=0), "z", jnp.float32)


def scatter_b(grads):
    own = fold(grads, "c", jnp.bfloat16)
    own = fold(jnp.moveaxis(own, 2, 0), "z", jnp.bfloat16)
    own = fold(own, "y", jnp.bfloat16)
    return fold(own, "x", jnp.float32)


def body(
    residual_in, cotangent, qkv_weight, out_weight, mlp_weight, norm_gains, seq_offsets, positions
):
    token_count, model_width = residual_in.shape
    head_dim = HEAD_DIM
    head_count = HEADS
    query_width = head_count * head_dim
    reach_count = max(1, WINDOW // token_count)
    halo_rows = reach_count * token_count
    query_block = min(token_count, 256)
    sizes = [(name, lax.axis_size(name)) for name in AXES]
    chips = sizes[0][1] * sizes[1][1]
    cores, fast = sizes[2][1], sizes[3][1]
    qkv_rows, out_rows, mlp_rows = qkv_weight.shape[0], out_weight.shape[0], mlp_weight.shape[0]
    gain_count = norm_gains.shape[0]
    halo_message = jnp.concatenate(
        [
            residual_in,
            jnp.pad(
                jnp.stack([positions // 256, positions % 256]).astype(jnp.bfloat16),
                ((0, 6), (0, model_width - token_count)),
            ),
        ],
        axis=0,
    )
    halo_parts = [shifted(halo_message, AXES, d) for d in range(reach_count, 0, -1)]
    gain_row = jnp.pad(norm_gains, (0, model_width - gain_count))[None]
    first = lax.all_gather(jnp.concatenate([qkv_weight, gain_row], axis=0), "z")
    first = lax.all_gather(first, ("y", "x"))
    first = spread(first, "c")
    core = lax.axis_index("c")
    first = jnp.take(first, lax.rem(core - jnp.arange(cores) + cores, cores), axis=0)
    first = jnp.moveaxis(first, 0, 1)
    qkv_full = first[:, :, :, :qkv_rows].reshape(-1, model_width)
    gain_full = first[:, :, :, qkv_rows, :gain_count].reshape(-1)
    shard_a = jnp.concatenate(
        [mlp_weight[:, :model_width], mlp_weight[:, model_width : 2 * model_width], out_weight], axis=0
    )
    full_a, full_b = gather_late(shard_a, mlp_weight[:, 2 * model_width :])
    rel = order_of([sizes[2], sizes[0], sizes[1], sizes[3]], True)
    count = cores * chips * fast
    flat_a = full_a.reshape(count, -1, model_width)
    gate_w = flat_a[:, :mlp_rows].reshape(-1, model_width)
    up_w = flat_a[:, mlp_rows : 2 * mlp_rows].reshape(-1, model_width)
    down_w = full_b.reshape(-1, model_width)
    out_full = jnp.take(flat_a[:, 2 * mlp_rows :], rel, axis=0)
    out_full = jnp.moveaxis(out_full.reshape(cores, chips, fast, out_rows, model_width), 0, 1).reshape(-1, model_width)
    gain_vals = gain_full.astype(jnp.float32)
    gain_in = gain_vals[0:model_width]
    gain_post = gain_vals[model_width : 2 * model_width]
    gain_pre = gain_vals[2 * model_width : 3 * model_width]
    gain_ff = gain_vals[3 * model_width : 4 * model_width]
    gain_query = gain_vals[4 * model_width : 4 * model_width + head_dim]
    gain_key = gain_vals[4 * model_width + head_dim :]
    input_f32 = residual_in.astype(jnp.float32)
    normed_in, rms_in = norm_rows(input_f32, gain_in)
    normed_in = normed_in.astype(jnp.bfloat16)
    projected_qkv = jnp.dot(normed_in, qkv_full.T, preferred_element_type=jnp.float32)
    query_raw = projected_qkv[:, :query_width].reshape(token_count, head_count, head_dim)
    key_raw = projected_qkv[:, query_width : query_width + head_dim]
    value_raw = projected_qkv[:, query_width + head_dim :]
    query_norm, rms_query = norm_rows(query_raw, gain_query)
    key_norm, rms_key = norm_rows(key_raw, gain_key)
    halo = jnp.stack(halo_parts)
    halo_pos = (halo[:, token_count, :token_count].astype(jnp.int32) * 256 + halo[:, token_count + 1, :token_count].astype(jnp.int32)).reshape(-1)
    cosine, sine_table = rope_tables(positions, head_dim)
    halo_cos, halo_sin = rope_tables(halo_pos, head_dim)
    halo_x = halo[:, :token_count].reshape(-1, model_width).astype(jnp.float32)
    halo_normed = norm_rows(halo_x, gain_in)[0].astype(jnp.bfloat16)
    halo_kv = jnp.dot(halo_normed, qkv_full[query_width:].T, preferred_element_type=jnp.float32)
    halo_key = rotate(norm_rows(halo_kv[:, :head_dim], gain_key)[0][:, None], halo_cos, halo_sin)[:, 0]
    halo_kv = jnp.concatenate([halo_key, halo_kv[:, head_dim:]], axis=1).astype(jnp.bfloat16)
    queries = (
        rotate(query_norm, cosine, sine_table)
        .reshape(token_count, query_width)
        .astype(jnp.bfloat16)
    )
    key_rot = rotate(key_norm[:, None, :], cosine, sine_table)[:, 0, :]
    own_kv = jnp.concatenate([key_rot, value_raw], axis=1).astype(jnp.bfloat16)
    all_kv = jnp.concatenate([halo_kv, own_kv], axis=0)
    attended_blk, total_blk = attend(queries, all_kv, seq_offsets, head_dim)
    projected = jnp.dot(attended_blk, out_full, preferred_element_type=jnp.float32)
    branch, rms_post = norm_rows(projected, gain_post)
    midstream = input_f32 + branch
    normed_mid, rms_mid = norm_rows(midstream, gain_pre)
    normed_mid = normed_mid.astype(jnp.bfloat16)
    gate_out = jnp.dot(normed_mid, gate_w.T, preferred_element_type=jnp.float32)
    up_out = jnp.dot(normed_mid, up_w.T, preferred_element_type=jnp.float32)
    activated = gelu_value(gate_out)
    hidden = (activated * up_out).astype(jnp.bfloat16)
    mlp_out = jnp.dot(hidden, down_w, preferred_element_type=jnp.float32)
    ff_branch, rms_ff = norm_rows(mlp_out, gain_ff)
    block_out = (midstream + ff_branch).astype(jnp.bfloat16)
    grad_mlp_out, term_ff = norm_back(mlp_out, rms_ff, gain_ff, cotangent)
    grad_mlp_b = grad_mlp_out.astype(jnp.bfloat16)
    shape_b = (cores, sizes[0][1], sizes[1][1], fast, -1, model_width)
    down_term = jnp.dot(hidden.T, grad_mlp_b, preferred_element_type=jnp.float32).astype(jnp.bfloat16)
    grad_down = scatter_b(down_term.reshape(shape_b))
    grad_hidden = jnp.dot(grad_mlp_b, down_w.T, preferred_element_type=jnp.float32)
    grad_gate = (grad_hidden * up_out * gelu_slope(gate_out)).astype(jnp.bfloat16)
    grad_up = (grad_hidden * activated).astype(jnp.bfloat16)
    grad_mid = jnp.dot(grad_gate, gate_w, preferred_element_type=jnp.float32) + jnp.dot(
        grad_up, up_w, preferred_element_type=jnp.float32
    )
    gate_term = jnp.dot(grad_gate.T, normed_mid, preferred_element_type=jnp.float32).astype(jnp.bfloat16)
    up_term = jnp.dot(grad_up.T, normed_mid, preferred_element_type=jnp.float32).astype(jnp.bfloat16)
    grad_mid_in, term_pre = norm_back(midstream, rms_mid, gain_pre, grad_mid)
    grad_midstream = cotangent + grad_mid_in
    grad_proj, term_post = norm_back(projected, rms_post, gain_post, grad_midstream)
    grad_proj_b = grad_proj.astype(jnp.bfloat16)
    grad_attended = jnp.dot(grad_proj_b, out_full.T, preferred_element_type=jnp.float32).astype(
        jnp.bfloat16
    )
    out_term = jnp.dot(attended_blk.T, grad_proj_b, preferred_element_type=jnp.float32).astype(jnp.bfloat16)
    out_term = jnp.moveaxis(out_term.reshape(chips, cores, fast, out_rows, model_width), 1, 0)
    out_term = jnp.take(out_term.reshape(count, out_rows, model_width), rel, axis=0)
    term_a = jnp.concatenate(
        [gate_term.reshape(count, mlp_rows, -1), up_term.reshape(count, mlp_rows, -1), out_term], axis=1
    )
    grad_a = scatter_a(term_a.reshape(shape_b))
    grad_mlp = jnp.concatenate([grad_a[:mlp_rows], grad_a[mlp_rows : 2 * mlp_rows], grad_down], axis=1)
    grad_out = grad_a[2 * mlp_rows :]
    grad_kv = jnp.zeros((halo_rows + token_count, 2 * head_dim), jnp.float32)
    key_start = halo_rows - WINDOW
    grad_q_blk, grad_kv_blk = attend_back(
        queries, all_kv, seq_offsets, total_blk, grad_attended, head_dim
    )
    grad_kv = grad_kv.at[key_start : key_start + WINDOW + query_block].add(grad_kv_blk)
    own_grad = grad_kv[halo_rows:]
    for distance in range(1, reach_count + 1):
        part_start = (reach_count - distance) * token_count
        own_grad = own_grad + shifted(
            grad_kv[part_start : part_start + token_count].astype(jnp.bfloat16),
            AXES,
            -distance,
        ).astype(jnp.float32)
    grad_query = grad_q_blk.reshape(token_count, head_count, head_dim)
    grad_qnorm = unrotate(grad_query, cosine, sine_table)
    grad_qraw, term_query = norm_back(query_raw, rms_query, gain_query, grad_qnorm)
    grad_knorm = unrotate(own_grad[:, None, :head_dim], cosine, sine_table)[:, 0, :]
    grad_kraw, term_key = norm_back(key_raw, rms_key, gain_key, grad_knorm)
    grad_qkv_b = jnp.concatenate(
        [grad_qraw.reshape(token_count, query_width), grad_kraw, own_grad[:, head_dim:]], axis=1
    ).astype(jnp.bfloat16)
    grad_normed = jnp.dot(grad_qkv_b, qkv_full, preferred_element_type=jnp.float32)
    grad_in_norm, term_in = norm_back(input_f32, rms_in, gain_in, grad_normed)
    grad_input = grad_midstream + grad_in_norm
    gain_term = jnp.concatenate(
        [
            jnp.sum(term_in, axis=0),
            jnp.sum(term_post, axis=0),
            jnp.sum(term_pre, axis=0),
            jnp.sum(term_ff, axis=0),
            jnp.sum(term_query, axis=(0, 1)),
            jnp.sum(term_key, axis=0),
        ]
    )
    qkv_term = jnp.dot(grad_qkv_b.T, normed_in, preferred_element_type=jnp.float32).astype(jnp.bfloat16)
    gain_rows = jnp.pad(gain_term.astype(jnp.bfloat16).reshape(count, 1, gain_count), ((0, 0), (0, 7), (0, model_width - gain_count)))
    last = jnp.concatenate([qkv_term.reshape(count, qkv_rows, model_width), gain_rows], axis=1)
    last = jnp.moveaxis(last.reshape(chips, cores, fast, -1, model_width), 1, 0)
    last = jnp.take(last.reshape(count, -1, model_width), rel, axis=0)
    last = scatter_a(last.reshape(shape_b))
    grad_qkv, grad_gains = last[:qkv_rows], last[qkv_rows, :gain_count]
    return (block_out, grad_input, grad_qkv, grad_out, grad_mlp, grad_gains)


def solution(mesh):
    in_specs = (
        P(AXES, None),
        P(AXES, None),
        P(AXES, None),
        P(AXES, None),
        P(AXES, None),
        P(AXES),
        P(AXES),
        P(AXES),
    )
    out_specs = (
        P(AXES, None),
        P(AXES, None),
        P(AXES, None),
        P(AXES, None),
        P(AXES, None),
        P(AXES),
    )
    return jax.shard_map(body, mesh=split_mesh(mesh), in_specs=in_specs, out_specs=out_specs, check_vma=False)
```

```python
import functools
import math

import jax
import jax.numpy as jnp
from jax import lax
from jax.experimental import pallas as pl
from jax.experimental.pallas import tpu as pltpu
from jax.sharding import Mesh, PartitionSpec as P

HEADS = 4
HEAD_DIM = 256
WINDOW = 512
EPSILON = 1e-06
ROPE_BASE = 10000.0
GELU_SCALE = 0.7978845608028654
GELU_CUBIC = 0.044715

AXES = ("y", "x", "c", "z")
BF = jnp.bfloat16
F32 = jnp.float32
VMEM = pl.BlockSpec(memory_space=pltpu.VMEM)
SMEM = pl.BlockSpec(memory_space=pltpu.SMEM)


def split_mesh(mesh):
    slow, fast = mesh.devices.shape
    cores = 2 if slow % 2 == 0 else 1
    chips = slow // cores
    across = max(d for d in range(1, math.isqrt(chips) + 1) if chips % d == 0)
    return Mesh(mesh.devices.reshape(chips // across, across, cores, fast), AXES)


def pass_on(block, axis, step):
    count = lax.axis_size(axis)
    return lax.ppermute(block, axis, [(i, (i + step) % count) for i in range(count)])


def shifted(block, distance):
    count = math.prod(lax.axis_size(name) for name in AXES)
    route = [(i - distance, i) for i in range(count) if 0 <= i - distance < count]
    return lax.ppermute(block, AXES, route)


def spread(block, axis):
    return [block] + [pass_on(block, axis, d) for d in range(1, lax.axis_size(axis))]


def after(value, *others):
    return lax.optimization_barrier((value, *others))[0]


def spread_z(shard):
    far = spread(shard, "z")
    half = len(far) // 2
    return jnp.stack(far[:half]), jnp.stack(far[half:])


def spread_xy(halves):
    low, high = halves
    half, rest = low.shape[0], high.shape[0]
    tail = low.shape[1:]
    low_x = spread(low, "x")
    high_y = spread(high, "y")
    nx, ny = len(low_x), len(high_y)
    low_all = spread(jnp.stack(low_x), "y")
    high_all = spread(jnp.stack(high_y), "x")
    pieces = []
    for y, piece in enumerate(low_all):
        coords = [(y, x, z) for x in range(nx) for z in range(half)]
        pieces.append((piece.reshape(-1, *tail), coords))
    for x, piece in enumerate(high_all):
        coords = [(y, x, half + z) for y in range(ny) for z in range(rest)]
        pieces.append((piece.reshape(-1, *tail), coords))
    full = []
    for piece, coords in pieces:
        for c, part in enumerate(spread(piece, "c")):
            full.append((part, [(c, *coord) for coord in coords]))
    return full


def total(parts):
    return functools.reduce(lambda a, b: a + b, [p.astype(F32) for p in parts])


def fold(parts, axis):
    arrived = []
    for d in range(1, lax.axis_size(axis)):
        arrived.append(pass_on(total([p[d] for p in parts]).astype(BF), axis, -d))
    return [p[0] for p in parts] + arrived


def grad_coords(ny, nx, nz):
    half = nz // 2
    low = [(y, x, z) for x in range(nx) for y in range(ny) for z in range(half)]
    high = [(y, x, z) for y in range(ny) for x in range(nx) for z in range(half, nz)]
    return low, high


def scatter(lows, highs, sizes):
    ny, nx, nc, nz = sizes
    half = nz // 2
    tail = lows[0].shape[1:]
    low = [lows[0]] + [pass_on(lows[d], "c", -d) for d in range(1, nc)]
    high = [highs[0]] + [pass_on(highs[d], "c", -d) for d in range(1, nc)]
    low = [p.reshape(nx, ny, half, *tail) for p in low]
    high = [p.reshape(ny, nx, nz - half, *tail) for p in high]
    low, high = fold(low, "x"), fold(high, "y")
    low, high = fold(low, "y"), fold(high, "x")
    arrived = []
    for d in range(1, nz):
        source = [p[d] for p in low] if d < half else [p[d - half] for p in high]
        arrived.append(pass_on(total(source).astype(BF), "z", -d))
    return total([p[0] for p in low] + arrived)


def dot_nn(a, b):
    return lax.dot_general(a, b, (((1,), (0,)), ((), ())), preferred_element_type=F32)


def dot_nt(a, b):
    return lax.dot_general(a, b, (((1,), (1,)), ((), ())), preferred_element_type=F32)


def dot_tn(a, b):
    return lax.dot_general(a, b, (((0,), (0,)), ((), ())), preferred_element_type=F32)


def inverse_rms(values):
    return lax.rsqrt(jnp.mean(values * values, axis=-1, keepdims=True) + EPSILON)


def norm_back(values, inv_rms, gain_plus, upstream):
    weighted = upstream * gain_plus
    inner = jnp.mean(weighted * values, axis=-1, keepdims=True)
    grad = inv_rms * weighted - values * (inv_rms * inv_rms * inv_rms) * inner
    return grad, jnp.sum(upstream * values * inv_rms, axis=0, keepdims=True)


def turn(values, cosine, sine):
    half = values.shape[-1] // 2
    first, second = values[:, :half], values[:, half:]
    return jnp.concatenate([first * cosine - second * sine, second * cosine + first * sine], axis=-1)


def call(body, name, outs, args, flops, specs=None, scratch=(), grid=()):
    size = sum(math.prod(a.shape) * a.dtype.itemsize for a in list(args) + list(outs))
    return pl.pallas_call(
        body,
        name=name,
        grid=grid,
        out_shape=outs,
        in_specs=specs or [VMEM] * len(args),
        out_specs=[VMEM] * len(outs),
        scratch_shapes=list(scratch),
        compiler_params=pltpu.CompilerParams(vmem_limit_bytes=60 << 20),
        cost_estimate=pl.CostEstimate(flops=int(flops), bytes_accessed=int(size), transcendentals=0),
    )(*args)


def shape(dims, dtype):
    return jax.ShapeDtypeStruct(dims, dtype)


def place_back(mine, relative, count):
    place = mine - relative
    return jnp.where(place < 0, place + count, place)


def absolute(place_ref, coord, sizes):
    ny, nx, nc, nz = sizes
    c, y, x, z = coord
    ay = place_back(place_ref[0], y, ny)
    ax = place_back(place_ref[1], x, nx)
    ac = place_back(place_ref[2], c, nc)
    az = place_back(place_ref[3], z, nz)
    return ((ay * nx + ax) * nc + ac) * nz + az


def front_kernel(cfg, place_ref, *refs):
    sizes, rows, aligned = cfg
    ny, nx, nc, nz = sizes
    count = nc if aligned else 1
    pieces, refs = refs[:count], refs[count:]
    halo_ref, x_ref, gain_ref, cos_ref, sin_ref = refs[:5]
    w_ref, normed_ref, raw_q_ref, raw_k_ref, q_ref, k_ref, v_ref = refs[5:]
    if aligned:
        for c, piece in enumerate(pieces):
            core = place_back(place_ref[2], c, nc)
            for chip in range(ny * nx):
                for z in range(nz):
                    start = pl.multiple_of(((chip * nc + core) * nz + z) * rows, 16)
                    w_ref[pl.ds(start, rows), :] = piece[chip * nz + z, :rows, :]
    else:
        w_ref[...] = pieces[0][...]
    tokens = x_ref.shape[0]
    head = q_ref.shape[-1]
    width = q_ref.shape[0] * head
    gain_in = 1.0 + gain_ref[0:1, :]
    gain_q = 1.0 + gain_ref[4:5, :head]
    gain_k = 1.0 + gain_ref[5:6, :head]
    values = x_ref[...].astype(F32)
    normed = (values * inverse_rms(values) * gain_in).astype(BF)
    normed_ref[...] = normed
    halo = halo_ref[...].astype(F32)
    halo = (halo * inverse_rms(halo) * gain_in).astype(BF)
    behind = halo.shape[0]
    raw = dot_nt(normed, w_ref[width:, :])
    far = dot_nt(halo, w_ref[width:, :])
    raw_k_ref[...] = raw[:, :head]
    v_ref[:behind, :] = far[:, head:].astype(BF)
    v_ref[behind:, :] = raw[:, head:].astype(BF)
    far_k, own_k = far[:, :head], raw[:, :head]
    far_k = far_k * inverse_rms(far_k) * gain_k
    own_k = own_k * inverse_rms(own_k) * gain_k
    k_ref[:behind, :] = turn(far_k, cos_ref[:behind, :], sin_ref[:behind, :]).astype(BF)
    cosine, sine = cos_ref[behind:, :], sin_ref[behind:, :]
    k_ref[behind:, :] = turn(own_k, cosine, sine).astype(BF)
    for h in range(q_ref.shape[0]):
        columns = slice(h * head, (h + 1) * head)
        raw_q = dot_nt(normed, w_ref[columns, :])
        raw_q_ref[:, columns] = raw_q
        q_ref[h] = turn(raw_q * inverse_rms(raw_q) * gain_q, cosine, sine).astype(BF)


def attend_kernel(q_ref, k_ref, v_ref, offset_ref, p_ref, att_ref):
    heads, tokens, head = q_ref.shape
    keys = k_ref.shape[0]
    row = lax.broadcasted_iota(jnp.int32, (tokens, keys), 0)
    col = lax.broadcasted_iota(jnp.int32, (tokens, keys), 1)
    distance = row + (keys - tokens) - col
    visible = (distance >= 0) & (distance < WINDOW) & (distance <= offset_ref[...])
    for h in range(heads):
        scores = dot_nt(q_ref[h], k_ref[...]) * head ** (-0.5)
        weight = jnp.where(visible, jnp.exp(scores), 0.0)
        probs = (weight * (1.0 / jnp.sum(weight, axis=-1, keepdims=True))).astype(BF)
        p_ref[h] = probs
        att_ref[:, h * head : (h + 1) * head] = dot_nn(probs, v_ref[...]).astype(BF)


def middle_kernel(cfg, place_ref, *refs):
    sizes, rows, coords, aligned = cfg
    pieces, refs = refs[: len(coords)], refs[len(coords) :]
    att_ref, x_ref, gain_ref, w_ref, projected_ref, mid_ref, normed_ref = refs
    if aligned:
        for piece, blocks in zip(pieces, coords):
            for i, coord in enumerate(blocks):
                start = pl.multiple_of(absolute(place_ref, coord, sizes) * rows, 16)
                w_ref[pl.ds(start, rows), :] = piece[i]
    else:
        w_ref[...] = pieces[0][...]
    projected = dot_nn(att_ref[...], w_ref[...])
    projected_ref[...] = projected
    mid = x_ref[...].astype(F32) + projected * inverse_rms(projected) * (1.0 + gain_ref[1:2, :])
    mid_ref[...] = mid
    normed_ref[...] = (mid * inverse_rms(mid) * (1.0 + gain_ref[2:3, :])).astype(BF)


def mlp_kernel(cfg, place_ref, *refs):
    sizes, mlp_rows, out_rows, coords, grads, aligned = cfg
    n = len(coords)
    a_refs, b_refs, refs = refs[:n], refs[n : 2 * n], refs[2 * n :]
    normed_ref, mid_ref, projected_ref, cot_ref, gain_ref, att_ref, out_w_ref = refs[:7]
    block_ref, gmid_ref, gatt_ref, term_ref = refs[7:11]
    refs = refs[11:]
    m = len(grads)
    ga_refs, gb_refs, refs = refs[:m], refs[m : 2 * m], refs[2 * m :]
    gate_w, up_w, down_w, hidden_ref, act_ref, slope_ref = refs
    blocks = [coord for piece in coords for coord in piece]
    if aligned:
        position = 0
        for a_ref, b_ref, piece in zip(a_refs, b_refs, coords):
            for i in range(len(piece)):
                here = slice(position * mlp_rows, (position + 1) * mlp_rows)
                gate_w[here, :] = a_ref[i, :mlp_rows, :]
                up_w[here, :] = a_ref[i, mlp_rows : 2 * mlp_rows, :]
                down_w[here, :] = b_ref[i]
                position += 1
    else:
        gate_w[...] = a_refs[0][0]
        up_w[...] = a_refs[0][1]
        down_w[...] = b_refs[0][...]
    where_of = {coord: (g, i) for g, piece in enumerate(grads) for i, coord in enumerate(piece)}
    normed = normed_ref[...]
    width = gate_w.shape[0]
    tile = 256
    mlp_out = None
    for j in range(width // tile):
        here = slice(j * tile, (j + 1) * tile)
        gate = dot_nt(normed, gate_w[here, :])
        up = dot_nt(normed, up_w[here, :])
        square = gate * gate
        tangent = jnp.tanh(GELU_SCALE * gate * (1.0 + GELU_CUBIC * square))
        active = 0.5 * gate * (1.0 + tangent)
        slope = 0.5 * (1.0 + tangent) + 0.5 * gate * (1.0 - tangent * tangent) * GELU_SCALE * (
            1.0 + 3.0 * GELU_CUBIC * square
        )
        hidden = (active * up).astype(BF)
        act_ref[:, here] = active
        slope_ref[:, here] = slope * up
        hidden_ref[:, here] = hidden
        part = dot_nn(hidden, down_w[here, :])
        mlp_out = part if mlp_out is None else mlp_out + part
    gain_ff = 1.0 + gain_ref[3:4, :]
    cot = cot_ref[...]
    mid = mid_ref[...]
    inv_ff = inverse_rms(mlp_out)
    block_ref[...] = (mid + mlp_out * inv_ff * gain_ff).astype(BF)
    grad_out, term_ff = norm_back(mlp_out, inv_ff, gain_ff, cot)
    grad_out = grad_out.astype(BF)
    grad_mid = None
    for j in range(width // tile):
        here = slice(j * tile, (j + 1) * tile)
        grad_hidden = dot_nt(grad_out, down_w[here, :])
        grad_gate = (grad_hidden * slope_ref[:, here]).astype(BF)
        grad_up = (grad_hidden * act_ref[:, here]).astype(BF)
        part = dot_nn(grad_gate, gate_w[here, :]) + dot_nn(grad_up, up_w[here, :])
        grad_mid = part if grad_mid is None else grad_mid + part
        d_gate = dot_tn(grad_gate, normed).astype(BF)
        d_up = dot_tn(grad_up, normed).astype(BF)
        d_down = dot_tn(hidden_ref[:, here], grad_out).astype(BF)
        if aligned:
            for b in range(tile // mlp_rows):
                g, i = where_of[blocks[j * (tile // mlp_rows) + b]]
                part = slice(b * mlp_rows, (b + 1) * mlp_rows)
                ga_refs[g][i, :mlp_rows, :] = d_gate[part]
                ga_refs[g][i, mlp_rows : 2 * mlp_rows, :] = d_up[part]
                gb_refs[g][i] = d_down[part]
        else:
            ga_refs[0][0, here, :] = d_gate
            ga_refs[0][1, here, :] = d_up
            gb_refs[0][here, :] = d_down
    gain_pre = 1.0 + gain_ref[2:3, :]
    grad_in, term_pre = norm_back(mid, inverse_rms(mid), gain_pre, grad_mid)
    grad_mid = cot + grad_in
    gmid_ref[...] = grad_mid
    projected = projected_ref[...]
    grad_proj, term_post = norm_back(projected, inverse_rms(projected), 1.0 + gain_ref[1:2, :], grad_mid)
    grad_proj = grad_proj.astype(BF)
    term_ref[...] = jnp.concatenate([term_post, term_pre, term_ff, jnp.zeros((5, term_ff.shape[1]), F32)], axis=0)
    head = gatt_ref.shape[-1]
    for h in range(gatt_ref.shape[0]):
        gatt_ref[h] = dot_nt(grad_proj, out_w_ref[h * head : (h + 1) * head, :]).astype(BF)
    d_out = dot_tn(att_ref[...], grad_proj).astype(BF)
    if aligned:
        hidden_rows = d_out.shape[0]
        out_scratch = down_w
        out_scratch[:hidden_rows, :] = d_out
        for g, piece in enumerate(grads):
            for i, coord in enumerate(piece):
                start = pl.multiple_of(absolute(place_ref, coord, sizes) * out_rows, 16)
                ga_refs[g][i, 2 * mlp_rows :, :] = out_scratch[pl.ds(start, out_rows), :]
    else:
        ga_refs[1][...] = d_out


def attend_back_kernel(
    p_ref, gatt_ref, q_ref, k_ref, v_ref, raw_ref, cos_ref, sin_ref, gain_ref, dq_ref, far_ref, own_ref, term_ref
):
    heads, tokens, head = q_ref.shape
    keys = k_ref.shape[0]
    cosine, sine = cos_ref[keys - tokens :, :], sin_ref[keys - tokens :, :]
    gain = 1.0 + gain_ref[4:5, :head]
    scale = head ** (-0.5)
    d_keys = d_values = term = None
    for h in range(heads):
        upstream = gatt_ref[h]
        low = p_ref[h]
        probs = low.astype(F32)
        grad_probs = dot_nt(upstream, v_ref[...])
        delta = jnp.sum(probs * grad_probs, axis=-1, keepdims=True)
        grad_scores = (probs * (grad_probs - delta) * scale).astype(BF)
        grad_query = dot_nn(grad_scores, k_ref[...])
        key_part = dot_tn(grad_scores, q_ref[h])
        value_part = dot_tn(low, upstream)
        d_keys = key_part if d_keys is None else d_keys + key_part
        d_values = value_part if d_values is None else d_values + value_part
        raw = raw_ref[:, h * head : (h + 1) * head]
        grad, term_h = norm_back(raw, inverse_rms(raw), gain, turn(grad_query, cosine, -sine))
        dq_ref[:, h * head : (h + 1) * head] = grad.astype(BF)
        term = term_h if term is None else term + term_h
    behind = keys - tokens
    far_ref[:, :head] = d_keys[:behind].astype(BF)
    far_ref[:, head:] = d_values[:behind].astype(BF)
    own_ref[:, :head] = d_keys[behind:]
    own_ref[:, head:] = d_values[behind:]
    term_ref[...] = jnp.broadcast_to(term, term_ref.shape)


def query_back_kernel(dq_ref, normed_ref, w_ref, dw_ref, part_ref):
    width = dq_ref.shape[1]
    dw_ref[...] = dot_tn(dq_ref[...], normed_ref[...]).astype(BF)
    part_ref[...] = dot_nn(dq_ref[...], w_ref[:width, :])


def input_back_kernel(cfg, place_ref, *refs):
    sizes, rows, grads, aligned, gain_count, reach = cfg
    far_refs, refs = refs[:reach], refs[reach:]
    own_ref, raw_ref, cos_ref, sin_ref, gain_ref, normed_ref, w_ref, dwq_ref, part_ref, x_ref, gmid_ref = refs[:11]
    term_mid_ref, term_q_ref = refs[11:13]
    gin_ref = refs[13]
    outs, (dw_ref, vec_ref) = refs[14:-2], refs[-2:]
    tokens, head = raw_ref.shape
    behind = cos_ref.shape[0] - tokens
    cosine, sine = cos_ref[behind:, :], sin_ref[behind:, :]
    grad = own_ref[...]
    for far in far_refs:
        grad = grad + far[...].astype(F32)
    raw = raw_ref[...]
    d_key, term_k = norm_back(raw, inverse_rms(raw), 1.0 + gain_ref[5:6, :head], turn(grad[:, :head], cosine, -sine))
    both = jnp.concatenate([d_key, grad[:, head:]], axis=1).astype(BF)
    width = dwq_ref.shape[0]
    grad_normed = part_ref[...] + dot_nn(both, w_ref[width:, :])
    values = x_ref[...].astype(F32)
    grad_in, term_in = norm_back(values, inverse_rms(values), 1.0 + gain_ref[0:1, :], grad_normed)
    gin_ref[...] = gmid_ref[...] + grad_in
    dw_ref[:width, :] = dwq_ref[...]
    dw_ref[width:, :] = dot_tn(both, normed_ref[...]).astype(BF)
    model = values.shape[1]
    vec_ref[:, :model] = jnp.broadcast_to(term_in, (8, model))
    for i in range(3):
        vec_ref[:, (i + 1) * model : (i + 2) * model] = jnp.broadcast_to(term_mid_ref[i : i + 1, :], (8, model))
    vec_ref[:, 4 * model : 4 * model + head] = term_q_ref[...]
    vec_ref[:, 4 * model + head :] = jnp.broadcast_to(term_k, (8, head))
    if aligned:
        for number in range(math.prod(sizes)):
            rest, az = divmod(number, sizes[3])
            rest, ac = divmod(rest, sizes[2])
            ay, ax = divmod(rest, sizes[1])
            y = place_back(place_ref[0], ay, sizes[0])
            x = place_back(place_ref[1], ax, sizes[1])
            c = place_back(place_ref[2], ac, sizes[2])
            z = place_back(place_ref[3], az, sizes[3])
            half = sizes[3] // 2
            low = ((c * sizes[1] + x) * sizes[0] + y) * half + z
            high = ((c * sizes[0] + y) * sizes[1] + x) * (sizes[3] - half) + z - half
            weight = dw_ref[number * rows : (number + 1) * rows, :]
            gains = vec_ref[:, number * gain_count : (number + 1) * gain_count].astype(BF)
            for ref, index, here in ((outs[0], low, z < half), (outs[1], high, z >= half)):

                @pl.when(here)
                def _():
                    ref[index, :rows, :] = weight
                    ref[index, rows:, :gain_count] = gains
    else:
        outs[0][...] = dw_ref[...]
        outs[1][...] = vec_ref[...]


def relative_order(sizes):
    ny, nx, nc, nz = sizes
    index = jnp.zeros((), jnp.int32)
    axes = {"y": ny, "x": nx, "c": nc, "z": nz}
    place = {
        name: lax.rem(lax.axis_index(name) - jnp.arange(count, dtype=jnp.int32) + count, count)
        for name, count in axes.items()
    }
    grid = (
        (place["y"][None, :, None, None] * nx + place["x"][None, None, :, None]) * nc + place["c"][:, None, None, None]
    ) * nz + place["z"][None, None, None, :]
    return grid


def body(residual_in, cotangent, qkv_weight, out_weight, mlp_weight, norm_gains, seq_offsets, positions):
    tokens, model = residual_in.shape
    head = HEAD_DIM
    width = HEADS * head
    reach = max(1, WINDOW // tokens)
    sizes = tuple(lax.axis_size(name) for name in AXES)
    ny, nx, nc, nz = sizes
    count = math.prod(sizes)
    chips = ny * nx
    place = jnp.stack([lax.axis_index(name) for name in AXES]).astype(jnp.int32)
    qkv_rows, out_rows, mlp_rows = qkv_weight.shape[0], out_weight.shape[0], mlp_weight.shape[0]
    gain_count = norm_gains.shape[0]
    aligned = qkv_rows % 16 == 0 and out_rows % 16 == 0 and mlp_rows % 16 == 0 and nz % 2 == 0

    gain_row = jnp.pad(norm_gains, (0, model - gain_count))[None]
    first = jnp.concatenate([qkv_weight, gain_row], axis=0)
    shard_a = jnp.concatenate([mlp_weight[:, :model], mlp_weight[:, model : 2 * model], out_weight], axis=0)
    shard_b = mlp_weight[:, 2 * model :]
    packed = jnp.pad(
        jnp.stack([positions // 256, positions % 256]).astype(BF), ((0, 6), (0, model - tokens))
    )
    message = jnp.concatenate([residual_in, packed], axis=0)
    first = lax.all_gather(first, "z")
    halves_a = spread_z(after(shard_a, first))
    first = lax.all_gather(first, ("y", "x"))
    first = first.reshape(chips * nz, qkv_rows + 1, model)
    message = after(message, *halves_a)
    halo_parts = [shifted(message, d) for d in range(reach, 0, -1)]
    firsts = spread(first, "c")
    core = lax.axis_index("c")
    gains = jnp.stack([p[:, qkv_rows, :gain_count].reshape(chips, nz, gain_count) for p in firsts])
    gains = jnp.take(gains, lax.rem(core - jnp.arange(nc) + nc, nc), axis=0)
    gains = jnp.moveaxis(gains, 0, 1).reshape(-1).astype(F32)
    gain_rows = jnp.concatenate(
        [
            gains[: 4 * model].reshape(4, model),
            jnp.pad(gains[4 * model :].reshape(2, head), ((0, 2), (0, model - head))),
        ],
        axis=0,
    )
    pieces_a = spread_xy(halves_a)
    halves_b = spread_z(after(shard_b, *halo_parts))
    pieces_b = spread_xy(halves_b)

    halo = jnp.stack(halo_parts)
    halo_pos = halo[:, tokens, :tokens].astype(jnp.int32) * 256 + halo[:, tokens + 1, :tokens].astype(jnp.int32)
    all_pos = jnp.concatenate([halo_pos.reshape(-1), positions]).astype(F32)
    frequency = jnp.power(F32(ROPE_BASE), jnp.arange(head // 2, dtype=F32) * (-2.0 / head))
    angle = all_pos[:, None] * frequency[None, :]
    cosine, sine = jnp.cos(angle), jnp.sin(angle)
    halo_x = halo[:, :tokens].reshape(-1, model)
    keys = reach * tokens + tokens

    if aligned:
        weights = firsts
    else:
        flat = jnp.stack([p[:, :qkv_rows].reshape(chips, nz, qkv_rows, model) for p in firsts])
        flat = jnp.take(flat, lax.rem(core - jnp.arange(nc) + nc, nc), axis=0)
        weights = [jnp.moveaxis(flat, 0, 1).reshape(-1, model)]
    args = [place, *weights, halo_x, residual_in, gain_rows, cosine, sine]
    qkv_w, normed_in, raw_q, raw_k, q, k, v = call(
        functools.partial(front_kernel, (sizes, qkv_rows, aligned)),
        "front",
        [
            shape((count * qkv_rows, model), BF),
            shape((tokens, model), BF),
            shape((tokens, width), F32),
            shape((tokens, head), F32),
            shape((HEADS, tokens, head), BF),
            shape((keys, head), BF),
            shape((keys, head), BF),
        ],
        args,
        2 * tokens * model * (width + 6 * head),
        specs=[SMEM] + [VMEM] * (len(args) - 1),
    )
    probs, attended = call(
        attend_kernel,
        "attend",
        [shape((HEADS, tokens, keys), BF), shape((tokens, width), BF)],
        [q, k, v, seq_offsets[:, None]],
        4 * width * tokens * keys,
    )

    coords = [piece for _, piece in pieces_a]
    if aligned:
        middle_w = [p for p, _ in pieces_a]
        middle_specs = [
            pl.BlockSpec((p.shape[0], out_rows, model), lambda i: (0, 2 * mlp_rows // out_rows, 0)) for p in middle_w
        ]
        if 2 * mlp_rows % out_rows:
            raise ValueError("row blocks")
        a_args, b_args = middle_w, [p for p, _ in pieces_b]
    else:
        order = [coord for piece in coords for coord in piece]
        all_a = jnp.concatenate([p for p, _ in pieces_a], axis=0)
        all_b = jnp.concatenate([p for p, _ in pieces_b], axis=0)
        numbers = relative_order(sizes).reshape(-1)
        flat = [((c * ny + y) * nx + x) * nz + z for c, y, x, z in order]
        back = jnp.zeros((count,), jnp.int32).at[numbers[jnp.array(flat)]].set(jnp.arange(count, dtype=jnp.int32))
        middle_w = [jnp.take(all_a[:, 2 * mlp_rows :], back, axis=0).reshape(-1, model)]
        middle_specs = [VMEM]
        a_args = [
            jnp.stack(
                [
                    all_a[:, :mlp_rows].reshape(-1, model),
                    all_a[:, mlp_rows : 2 * mlp_rows].reshape(-1, model),
                ]
            )
        ]
        b_args = [all_b.reshape(-1, model)]
    coords_used = coords if aligned else [[None]]
    out_w, projected, midstream, normed_mid = call(
        functools.partial(middle_kernel, (sizes, out_rows, coords_used, aligned)),
        "middle",
        [
            shape((count * out_rows, model), BF),
            shape((tokens, model), F32),
            shape((tokens, model), F32),
            shape((tokens, model), BF),
        ],
        [place, *middle_w, attended, residual_in, gain_rows],
        2 * tokens * width * model,
        specs=[SMEM, *middle_specs, VMEM, VMEM, VMEM],
        grid=(1,) if aligned else (),
    )

    low, high = grad_coords(ny, nx, nz)
    per_core = len(low)
    grads = [[(c, *coord) for coord in part] for part in (low, high) for c in range(nc)]
    rows_a = 2 * mlp_rows + out_rows
    ff = count * mlp_rows
    if aligned:
        grad_shapes = [shape((len(g), rows_a, model), BF) for g in grads]
        grad_shapes += [shape((len(g), mlp_rows, model), BF) for g in grads]
        grads_used = grads
    else:
        grad_shapes = [shape((2, ff, model), BF), shape((width, model), BF), shape((ff, model), BF), shape((8, 128), BF)]
        grads_used = [[None], [None]]
    args = [place, *a_args, *b_args, normed_mid, midstream, projected, cotangent, gain_rows, attended, out_w]
    outs = call(
        functools.partial(mlp_kernel, (sizes, mlp_rows, out_rows, coords_used, grads_used, aligned)),
        "mlp",
        [
            shape((tokens, model), BF),
            shape((tokens, model), F32),
            shape((HEADS, tokens, head), BF),
            shape((8, model), F32),
            *grad_shapes,
        ],
        args,
        2 * tokens * model * (9 * ff + 2 * width),
        specs=[SMEM] + [VMEM] * (len(args) - 1),
        scratch=[pltpu.VMEM((ff, model), BF)] * 3
        + [pltpu.VMEM((tokens, ff), BF), pltpu.VMEM((tokens, ff), F32), pltpu.VMEM((tokens, ff), F32)],
    )
    block_out, grad_midstream, grad_att, term_mid = outs[:4]
    if aligned:
        terms = outs[4:]
        lows_a, highs_a = terms[:nc], terms[nc : 2 * nc]
        lows_b, highs_b = terms[2 * nc : 3 * nc], terms[3 * nc :]
    else:
        pair, d_out, d_down, _ = outs[4:]
        d_gate = pair[0].reshape(count, mlp_rows, model)
        d_up = pair[1].reshape(count, mlp_rows, model)
        d_down = d_down.reshape(count, mlp_rows, model)
        d_out = d_out.reshape(count, out_rows, model)
        where_of = {coord: i for i, coord in enumerate(order)}
        picks = [jnp.array([where_of[coord] for coord in g]) for g in grads]
        rel = relative_order(sizes).reshape(-1)
        rels = [rel[jnp.array([((c * ny + y) * nx + x) * nz + z for c, y, x, z in g])] for g in grads]
        a_terms = [jnp.concatenate([d_gate[i], d_up[i], d_out[r]], axis=1) for i, r in zip(picks, rels)]
        b_terms = [d_down[i] for i in picks]
        lows_a, highs_a, lows_b, highs_b = a_terms[:nc], a_terms[nc:], b_terms[:nc], b_terms[nc:]
    grad_down = scatter(lows_b, highs_b, sizes)
    grad_a = scatter(lows_a, highs_a, sizes)
    grad_mlp = jnp.concatenate([grad_a[:mlp_rows], grad_a[mlp_rows : 2 * mlp_rows], grad_down], axis=1)
    grad_out = grad_a[2 * mlp_rows :]

    d_query, far_grad, own_grad, term_q = call(
        attend_back_kernel,
        "attend_back",
        [
            shape((tokens, width), BF),
            shape((reach * tokens, 2 * head), BF),
            shape((tokens, 2 * head), F32),
            shape((8, head), F32),
        ],
        [probs, grad_att, q, k, v, raw_q, cosine, sine, gain_rows],
        10 * width * tokens * keys,
    )
    returned = []
    for distance in range(1, reach + 1):
        start = (reach - distance) * tokens
        returned.append(shifted(far_grad[start : start + tokens], -distance))
    dw_query, part = call(
        query_back_kernel,
        "query_back",
        [shape((width, model), BF), shape((tokens, model), F32)],
        [d_query, normed_in, qkv_w],
        4 * width * tokens * model,
    )
    if aligned:
        last_shapes = [shape((nc * per_core, qkv_rows + 8, model), BF)] * 2
    else:
        last_shapes = [shape((count * qkv_rows, model), BF), shape((8, count * gain_count), F32)]
    args = [
        place,
        *returned,
        own_grad,
        raw_k,
        cosine,
        sine,
        gain_rows,
        normed_in,
        qkv_w,
        dw_query,
        part,
        residual_in,
        grad_midstream,
        term_mid,
        term_q,
    ]
    grad_input, *last = call(
        functools.partial(input_back_kernel, (sizes, qkv_rows, grads, aligned, gain_count, reach)),
        "input_back",
        [shape((tokens, model), F32), *last_shapes],
        args,
        8 * head * tokens * model,
        specs=[SMEM] + [VMEM] * (len(args) - 1),
        scratch=[pltpu.VMEM((count * qkv_rows, model), BF), pltpu.VMEM((8, count * gain_count), F32)],
    )
    if aligned:
        lows = [last[0][c * per_core : (c + 1) * per_core] for c in range(nc)]
        highs = [last[1][c * per_core : (c + 1) * per_core] for c in range(nc)]
    else:
        gain_blocks = jnp.pad(
            last[1][0].astype(BF).reshape(count, 1, gain_count), ((0, 0), (0, 0), (0, model - gain_count))
        )
        last = jnp.concatenate([last[0].reshape(count, qkv_rows, model), gain_blocks], axis=1)
        lows, highs = [last[r] for r in rels[:nc]], [last[r] for r in rels[nc:]]
    last = scatter(lows, highs, sizes)
    grad_qkv, grad_gains = last[:qkv_rows], last[qkv_rows, :gain_count]
    return (block_out, grad_input, grad_qkv, grad_out, grad_mlp, grad_gains)


def solution(mesh):
    rows, flat = P(AXES, None), P(AXES)
    return jax.shard_map(
        body,
        mesh=split_mesh(mesh),
        in_specs=(rows, rows, rows, rows, rows, flat, flat, flat),
        out_specs=(rows, rows, rows, rows, rows, flat),
        check_vma=False,
    )
```
